256 devices in a mesh: gy: 4 (over x_lo, core), gx: 16 (over x_hi, z), rep: 4 (over y).
Axes of the slice: x: 4 (x_hi: 2, x_lo: 2; x = x_hi * 2 + x_lo), y: 4, z: 8, core: 2. Of those that a mesh axis runs over, the one named last changes fastest.
Arguments:
- pages: bfloat16 [4, 128, 512, 384], P('rep', 'gy', 'gx'), may hold values from -6 to 6
- cotangent: bfloat16 [4, 128, 512, 384], P('rep', 'gy', 'gx'), may hold values from -6 to 6
- conv_kernel: float32 [7, 7, 384], replicated, may hold values from -0.875 to 0.875
- conv_bias: float32 [384], replicated, may hold values from -3 to 3
- norm_gain: float32 [384], replicated, may hold values from 0.1 to 1.9
- norm_bias: float32 [384], replicated, may hold values from -3 to 3
- w_in: bfloat16 [1536, 384], replicated, may hold values from -0.3125 to 0.3125
- b_in: float32 [1536], replicated, may hold values from -3 to 3
- w_out: bfloat16 [384, 1536], replicated, may hold values from -0.15625 to 0.15625
- b_out: float32 [384], replicated, may hold values from -3 to 3
- layer_scale: float32 [384], replicated, may hold values from 0.2 to 2
Outputs:
- result: bfloat16 [4, 128, 512, 384], P('rep', 'gy', 'gx')
- grad_pages: bfloat16 [4, 128, 512, 384], P('rep', 'gy', 'gx')
- grad_kernel: float32 [7, 7, 384], replicated
- grad_conv_bias: float32 [384], replicated
- grad_gain: float32 [384], replicated
- grad_norm_bias: float32 [384], replicated
- grad_w_in: float32 [1536, 384], replicated
- grad_b_in: float32 [1536], replicated
- grad_w_out: float32 [384, 1536], replicated
- grad_b_out: float32 [384], replicated
- grad_scale: float32 [384], replicated
The draws below stay inside these ranges and needn't reach their ends.
All inputs are finite; a program needn't handle non-finite values.
Results may differ from the reference program's by a relative error of at most 0.0095.
Values may be sent and summed in bfloat16 or wider, within the bound.
A program may use at most 128 MiB of HBM per device.

```python
import math
import jax
import jax.numpy as jnp
from jax import lax

C = 384
HID = 1536
H = 128
W = 512
PAGES = 4
PIXELS = 262144


def shard_levels(rng, shape, pieces, low, top_value):
    loudness = 1.0
    for axis_at, parts in pieces:
        heights = jax.random.uniform(jax.random.fold_in(jax.random.fold_in(rng, 6), axis_at), (parts,), jnp.float32, low / len(pieces), top_value / len(pieces))
        loudness = loudness * jnp.repeat(jnp.exp(heights), shape[axis_at] // parts).reshape((-1,) + (1,) * (len(shape) - 1 - axis_at))
    return loudness


def noise(key, shape, deviation, bound, pieces=(), dtype=jnp.bfloat16):
    values = deviation * jax.random.normal(key, shape, jnp.float32)
    if pieces:
        values = values * shard_levels(key, shape, pieces, -0.22, 0.18)
    return jnp.clip(values, -bound, bound).astype(dtype)


def setup_inputs(seed: int = 0) -> dict:
    splits = jax.random.split(jax.random.key(seed), 12)
    return {
        "pages": noise(splits[0], (PAGES, H, W, C), 1.0, 6.0, ((0, 4), (1, 4), (2, 16))),
        "cotangent": noise(splits[1], (PAGES, H, W, C), 1.0, 6.0, ((0, 4), (1, 4), (2, 16))),
        "conv_kernel": noise(splits[2], (7, 7, C), 49 ** -0.5, 0.875, (), jnp.float32),
        "conv_bias": noise(splits[3], (C,), 0.5, 3.0, (), jnp.float32),
        "norm_gain": jnp.clip(1.0 + 0.18 * jax.random.normal(splits[4], (C,), jnp.float32), 0.1, 1.9),
        "norm_bias": noise(splits[5], (C,), 0.5, 3.0, (), jnp.float32),
        "w_in": noise(splits[6], (HID, C), C ** -0.5, 0.3125),
        "b_in": noise(splits[7], (HID,), 0.5, 3.0, (), jnp.float32),
        "w_out": noise(splits[8], (C, HID), HID ** -0.5, 0.15625),
        "b_out": noise(splits[9], (C,), 0.5, 3.0, (), jnp.float32),
        "layer_scale": jnp.clip(jnp.exp(jax.random.uniform(splits[10], (C,), jnp.float32, math.log(0.2), math.log(2.0))), 0.2, 2.0),
    }


norm_epsilon = 1e-06
inv_root_two = 0.7071067811865476
inv_root_tau = 0.3989422804014327

def gelu_grad(values):
    cdf = 0.5 * (1.0 + lax.erf(values * inv_root_two))
    pdf = jnp.exp(-0.5 * values * values) * inv_root_tau
    return cdf + values * pdf

def reference(pages, cotangent, conv_kernel, conv_bias, norm_gain, norm_bias, w_in, b_in, w_out, b_out, layer_scale):
    channels = pages.shape[3]

    def one_page(inputs):
        page, cot = inputs
        padded = jnp.pad(page, ((3, 3), (3, 3), (0, 0)))
        accum = jnp.zeros(page.shape, jnp.float32)
        for row_off in range(7):
            for col_off in range(7):
                accum = accum + padded[row_off:row_off + H, col_off:col_off + W, :].astype(jnp.float32) * conv_kernel[row_off, col_off]
        depth_out = accum + conv_bias
        average = lax.optimization_barrier(jnp.mean(depth_out, axis=-1, keepdims=True))
        centred = depth_out - average
        inv_std = lax.rsqrt(lax.optimization_barrier(jnp.mean(centred * centred, axis=-1, keepdims=True)) + norm_epsilon)
        normed = (centred * inv_std).reshape(-1, channels)
        inv_rows = inv_std.reshape(-1, 1)
        ln_out = (normed * norm_gain + norm_bias).astype(jnp.bfloat16)
        pre_act = lax.dot_general(ln_out, w_in, (((1,), (1,)), ((), ())), preferred_element_type=jnp.float32) + b_in
        hidden = jax.nn.gelu(pre_act, approximate=False).astype(jnp.bfloat16)
        branch = lax.dot_general(hidden, w_out, (((1,), (1,)), ((), ())), preferred_element_type=jnp.float32) + b_out
        page_rows = page.reshape(-1, channels).astype(jnp.float32)
        result = (page_rows + layer_scale * branch).astype(jnp.bfloat16).reshape(page.shape)
        cot_rows = cot.reshape(-1, channels).astype(jnp.float32)
        g_scale = lax.optimization_barrier(jnp.sum(cot_rows * branch, axis=0))
        d_branch32 = layer_scale * cot_rows
        g_bout = lax.optimization_barrier(jnp.sum(d_branch32, axis=0))
        d_branch = d_branch32.astype(jnp.bfloat16)
        g_wout = lax.dot_general(d_branch, hidden, (((0,), (0,)), ((), ())), preferred_element_type=jnp.float32)
        d_hidden = jnp.dot(d_branch, w_out, preferred_element_type=jnp.float32)
        d_pre32 = d_hidden * gelu_grad(pre_act)
        g_bin = lax.optimization_barrier(jnp.sum(d_pre32, axis=0))
        d_pre = d_pre32.astype(jnp.bfloat16)
        g_win = lax.dot_general(d_pre, ln_out, (((0,), (0,)), ((), ())), preferred_element_type=jnp.float32)
        d_norm = jnp.dot(d_pre, w_in, preferred_element_type=jnp.float32)
        g_gain = lax.optimization_barrier(jnp.sum(d_norm * normed, axis=0))
        g_nbias = lax.optimization_barrier(jnp.sum(d_norm, axis=0))
        d_scaled = d_norm * norm_gain
        d_depth32 = inv_rows * (d_scaled - lax.optimization_barrier(jnp.mean(d_scaled, axis=-1, keepdims=True)) - normed * lax.optimization_barrier(jnp.mean(d_scaled * normed, axis=-1, keepdims=True)))
        d_depth = d_depth32.astype(jnp.bfloat16).reshape(page.shape)
        depth_f = d_depth.astype(jnp.float32)
        g_cbias = lax.optimization_barrier(jnp.sum(depth_f, axis=(0, 1)))
        kernel_terms = []
        for row_off in range(7):
            for col_off in range(7):
                piece = padded[row_off:row_off + H, col_off:col_off + W, :].astype(jnp.float32)
                kernel_terms.append(lax.optimization_barrier(jnp.sum(depth_f * piece, axis=(0, 1))))
        g_kernel = jnp.stack(kernel_terms).reshape(7, 7, channels)
        grad_pad = jnp.pad(d_depth, ((3, 3), (3, 3), (0, 0)))
        back = jnp.zeros(page.shape, jnp.float32)
        for row_off in range(7):
            for col_off in range(7):
                back = back + grad_pad[6 - row_off:6 - row_off + H, 6 - col_off:6 - col_off + W, :].astype(jnp.float32) * conv_kernel[row_off, col_off]
        grad_page = (cot.astype(jnp.float32) + back).astype(jnp.bfloat16)
        return (result, grad_page, (g_kernel, g_cbias, g_gain, g_nbias, g_win, g_bin, g_wout, g_bout, g_scale))
    result, grad_pages, partials = lax.map(one_page, (pages, cotangent))
    factor = float(PIXELS) ** (-0.5)
    totals = [lax.optimization_barrier(jnp.sum(term, axis=0)) * factor for term in partials]
    return (result, grad_pages, totals[0], totals[1], totals[2], totals[3], totals[4], totals[5], totals[6], totals[7], totals[8])
```

```python
import functools

import jax
import jax.numpy as jnp
from jax import lax
from jax.experimental import pallas as pl
from jax.experimental.pallas import tpu as pltpu
from jax.sharding import PartitionSpec as P

norm_epsilon = 1e-06
inv_root_two = 0.7071067811865476
inv_root_tau = 0.3989422804014327

C = 384
HID = 1536
ROWS = 32
COLS = 32
PIX = ROWS * COLS
PW = 48
LB = 3
F32 = jnp.float32
BF16 = jnp.bfloat16
PTS = (2.0, 0.5, 4.0 / 3.0, 0.75)
NT = (((1,), (1,)), ((), ()))
NN = (((1,), (0,)), ((), ()))


def dot(a, b, dims):
    return lax.dot_general(a, b, dims, preferred_element_type=F32)


def monic(roots):
    c = [1.0]
    for r in roots:
        c = [(c[i - 1] if i > 0 else 0.0) - (r * c[i] if i < len(c) else 0.0) for i in range(len(c) + 1)]
    return c


SQ = [p * p for p in PTS]
ALL = monic(SQ)
REST = [monic([q for q in SQ if q != p * p]) for p in PTS]
SCALE = [1.0 / (2.0 * p * p * sum(c * (p * p) ** i for i, c in enumerate(r))) for p, r in zip(PTS, REST)]
SCALE0 = 1.0 / ALL[0]


def linear(coefs, values):
    total = None
    for c, v in zip(coefs, values):
        term = v if c == 1.0 else c * v
        total = term if total is None else total + term
    return total


def to_points(d):
    out = [linear(ALL, d[0:9:2])]
    for p, rest in zip(PTS, REST):
        even = linear(rest, d[2:9:2])
        odd = p * linear(rest, d[1:8:2])
        out += [even + odd, even - odd]
    return out + [linear(ALL, d[1:10:2])]


def taps_to_points(t):
    out = [SCALE0 * t[0]]
    for p, f in zip(PTS, SCALE):
        even = linear([f * p**i for i in range(0, len(t), 2)], t[0::2])
        odd = linear([f * p**i for i in range(1, len(t), 2)], t[1::2])
        out += [even + odd, even - odd]
    return out + [t[-1]]


def from_points(m, count):
    plus = [m[1 + 2 * i] + m[2 + 2 * i] for i in range(4)]
    minus = [m[1 + 2 * i] - m[2 + 2 * i] for i in range(4)]
    out = []
    for j in range(count):
        v = linear([p**j for p in PTS], minus if j % 2 else plus)
        out.append(v + m[0] if j == 0 else v + m[9] if j == count - 1 else v)
    return out


def body(
    factor,
    pages_at, cot_at, ck, cb1, gain1, nbias1, w_in_at, b_in1, w_out_at, b_out1, ls1,
    result_at, gpages_at, fwin_at, fwout_at, small_at,
    pages, cot, w_in, w_out, result, gpages, fwin, fwout, small, in_sems, out_sems, wout_sems,
    pf, xu, page, du, dep, norm, inv, cotp, ln, lnt, db, dbt, hid, dp, dhat, outp, kb, kh, khf, acc, accv, gsum, smf,
    tb_s, tb_r, lr_s, lr_r, cn_s, cn_r,
    bwin, bwout, r0, s0, r1, s1, r3,
    sm, t0, sa, t1, sb, t2, sc, t3,
    cb, gain, nbias, b_in, b_out, ls,
    halo_ss, halo_rs, s0_ss, s0_rs, s1_ss, s1_rs, s3_ss, s3_rs,
    gz_ss, gz_rs, ga_ss, ga_rs, gc_ss, gc_rs,
    m0_ss, m0_rs, m1_ss, m1_rs, m2_ss, m2_rs, m3_ss, m3_rs, m4_ss, m4_rs, m5_ss, m5_rs,
):
    loads = [
        pltpu.make_async_copy(src, dst, in_sems.at[i])
        for i, (src, dst) in enumerate(((pages_at, pages), (cot_at, cot), (w_in_at, w_in), (w_out_at, w_out)))
    ]
    for c in loads:
        c.start()
    gy = lax.axis_index("gy")
    gx = lax.axis_index("gx")
    y = lax.axis_index("rep")
    core = gy % 2
    x = (gx // 8) * 2 + gy // 2
    z = gx % 8

    def device(px, py, pz, pc):
        return ((px % 2) * 2 + pc, (px // 2) * 8 + pz, py)

    partner = device(x, y, z, 1 - core)
    for row, ref in ((cb, cb1), (gain, gain1), (nbias, nbias1), (b_in, b_in1), (b_out, b_out1), (ls, ls1)):
        row[...] = ref[...].reshape(1, ref.shape[0])

    def x_peer(d):
        return device((x + d) % 4, y, z, core)

    def y_peer(d):
        return device(x, (y + d) % 4, z, core)

    def z_peer(d):
        return device(x, y, (z + d) % 8, core)

    def halo_peer(dy, dxx):
        return ((gy + dy + 4) % 4, (gx + dxx + 16) % 16, y)

    def remote(src, dst, ssem, rsem, dev):
        return pltpu.make_async_remote_copy(
            src_ref=src, dst_ref=dst, send_sem=ssem, recv_sem=rsem,
            device_id=dev, device_id_type=pl.DeviceIdType.MESH,
        )

    around = [(-1, 0), (1, 0), (0, -1), (0, 1), (-1, -1), (-1, 1), (1, -1), (1, 1)]
    peers = [halo_peer(*o) for o in around] + [partner]
    barrier = pltpu.get_barrier_semaphore()
    for dev in peers:
        pl.semaphore_signal(barrier, inc=1, device_id=dev, device_id_type=pl.DeviceIdType.MESH)

    def greet(n, carry):
        db, dz = n // 8, n % 8
        for dev in (device(x, (y + db) % 4, (z + dz) % 8, core), device((x + db) % 4, y, (z + dz) % 8, core)):
            pl.semaphore_signal(barrier, inc=1, device_id=dev, device_id_type=pl.DeviceIdType.MESH)
        return carry

    lax.fori_loop(1, 32, greet, 0)

    def lanes(lb):
        return slice(lb * 128, lb * 128 + 128)

    def halo_copies(n):
        out = []
        for i, (dy, dxx) in enumerate(around):
            if dxx == 0:
                s = 0 if dy < 0 else 1
                src, dst = tb_s.at[n, s], tb_r.at[n, 1 - s]
            elif dy == 0:
                s = 0 if dxx < 0 else 1
                src, dst = lr_s.at[n, s], lr_r.at[n, 1 - s]
            else:
                s = 0 if dy < 0 else 1
                t = 0 if dxx < 0 else 1
                src, dst = cn_s.at[n, s, t], cn_r.at[n, 1 - s, 1 - t]
            out.append(remote(src, dst, halo_ss.at[n, i], halo_rs.at[n, i], halo_peer(dy, dxx)))
        return out

    def halo_pack(n):
        for lb in range(LB):
            for s in range(2):
                for j in range(3):
                    row = j + 29 * s
                    tb_s[n, s, j, :, lanes(lb)] = pf[lb, (8 + row) * PW + 8 : (8 + row) * PW + 40, :].astype(BF16)
                    col = j + 29 * s
                    lr_s[n, s, j, :, lanes(lb)] = pf[lb, pl.ds(8 * PW + 8 + col, 32, stride=PW), :].astype(BF16)
                    for t in range(2):
                        col = j + 29 * t
                        cn_s[n, s, t, j, :, lanes(lb)] = pf[
                            lb, pl.ds((8 + 24 * s) * PW + 8 + col, 8, stride=PW), :
                        ].astype(BF16)

    def halo_unpack(n):
        up, down, left, right = gy > 0, gy < 3, gx > 0, gx < 15
        vert = (up, down)
        horz = (left, right)
        for lb in range(LB):
            for s in range(2):
                for j in range(3):
                    row = j + 5 + 35 * s
                    v = tb_r[n, s, j, :, lanes(lb)].astype(F32)
                    pf[lb, row * PW + 8 : row * PW + 40, :] = jnp.where(vert[s], v, 0.0)
                    v = lr_r[n, s, j, :, lanes(lb)].astype(F32)
                    pf[lb, pl.ds(8 * PW + 5 + 35 * s + j, 32, stride=PW), :] = jnp.where(horz[s], v, 0.0)
                    for t in range(2):
                        v = cn_r[n, s, t, j, :, lanes(lb)].astype(F32)
                        pf[lb, pl.ds(40 * s * PW + 5 + 35 * t + j, 8, stride=PW), :] = jnp.where(
                            vert[s] & horz[t], v, 0.0
                        )

    def build_strips(dst, keep):
        def step(r, carry):
            base = (r + 5) * PW + 5
            for lb in range(LB):
                d = [pf[lb, pl.ds(base + q, 8, stride=4), :] for q in range(10)]
                if keep is not None:
                    for q in range(4):
                        keep[lb, r, q] = d[q + 3]
                for k, v in enumerate(to_points(d)):
                    dst[lb, r, k] = v
            return carry
        lax.fori_loop(0, 38, step, 0)

    def load_pages(i, carry):
        for lb in range(LB):
            pf[lb, pl.ds(pl.multiple_of((i + 8) * PW + 8, 8), 32), :] = pages[i, :, lanes(lb)].astype(F32)
        return carry

    loads[0].wait()
    lax.fori_loop(0, 32, load_pages, 0)
    halo_pack(0)
    pl.semaphore_wait(barrier, len(peers) + 62)
    first = halo_copies(0)
    for c in first:
        c.start()

    for t in range(49):
        kb[t] = jnp.broadcast_to(ck[t // 7, t % 7 : t % 7 + 1, :], (8, C))

    def kernel_points(a, carry):
        taps = [kb[a * 7 + b] for b in range(7)]
        for k, v in enumerate(taps_to_points(taps)):
            kh[a * 10 + k] = v
        for k, v in enumerate(taps_to_points(taps[::-1])):
            khf[(6 - a) * 10 + k] = v
        return carry

    lax.fori_loop(0, 7, kernel_points, 0)
    for j in range(9):
        acc[j] = jnp.zeros((8, C), F32)

    def load_cot(i, carry):
        for lb in range(LB):
            outp[lb, pl.ds(pl.multiple_of(i * 32, 8), 32), :] = cot[i, :, lanes(lb)].astype(F32)
            for q in range(4):
                cotp[pl.ds(pl.multiple_of(i * 32 + q * 8, 8), 8), lanes(lb)] = outp[
                    lb, pl.ds(i * 32 + q, 8, stride=4), :
                ]
        return carry

    loads[1].wait()
    lax.fori_loop(0, 32, load_cot, 0)

    def make_db(b, carry):
        rows = pl.ds(pl.multiple_of(b * 128, 128), 128)
        v = cotp[rows, :] * ls[...]
        acc[3] += jnp.sum(v.reshape(16, 8, C), axis=0)
        db[rows, :] = v.astype(BF16)
        dbt[:, rows] = v.T.astype(BF16)
        return carry

    lax.fori_loop(0, 8, make_db, 0)

    for c in first:
        c.wait_recv()
    halo_unpack(0)
    build_strips(xu, page)

    def conv_rows(src, taps, lb, i):
        total = None
        for a in range(7):
            term = src[lb, pl.ds(i + a, 2)] * taps[a * 10 : a * 10 + 10, :, lanes(lb)]
            total = term if total is None else total + term
        return from_points([total[:, k] for k in range(10)], 4)

    for lb in range(LB):
        def conv_step(h, carry, lb=lb):
            outs_at = conv_rows(xu, kh, lb, h * 2)
            for q in range(4):
                v = outs_at[q] + cb[:, lanes(lb)]
                for r in range(2):
                    dep[pl.ds(pl.multiple_of(h * 64 + r * 32 + q * 8, 8), 8), lanes(lb)] = v[r]
            return carry
        lax.fori_loop(0, 16, conv_step, 0)

    def norm_step(b, carry):
        rows = pl.ds(pl.multiple_of(b * 128, 128), 128)
        v = dep[rows, :]
        centred = v - jnp.mean(v, axis=-1, keepdims=True)
        istd = lax.rsqrt(jnp.mean(centred * centred, axis=-1, keepdims=True) + norm_epsilon)
        n = centred * istd
        norm[rows, :] = n
        inv[rows, :] = jnp.broadcast_to(istd, (128, 128))
        o = n * gain[...] + nbias[...]
        ln[rows, :] = o.astype(BF16)
        lnt[:, rows] = o.T.astype(BF16)
        return carry

    lax.fori_loop(0, 8, norm_step, 0)

    bufs = (bwin, bwout)
    a_at = (x, y)
    b_at = (y, x)
    a_peer = (x_peer, y_peer)
    b_peer = (y_peer, x_peer)

    def core_send(q, k):
        return remote(
            bufs[q].at[pl.ds(k * 48 + (1 - core) * 24, 24)], r0.at[q, k], s0_ss.at[q, k], s0_rs.at[q, k], partner
        )

    def a_send(q, k, d):
        return remote(
            s0.at[q, k, pl.ds(((a_at[q] + d) % 4) * 6, 6)], r1.at[q, d - 1, k],
            s1_ss.at[q, d - 1, k], s1_rs.at[q, d - 1, k], a_peer[q](d),
        )

    def plane(q, pb, pz):
        return device(x, pb, pz, core) if q == 0 else device(pb, y, pz, core)

    def p_send(q, k, g):
        owner = (k + g) % 4
        db, dz = (owner + 4 - b_at[q]) % 4, (g + 8 - z) % 8
        return remote(
            s1.at[q, k, g], r3.at[q, db, dz], s3_ss.at[q, k, g], s3_rs.at[q, db, dz], plane(q, owner, g)
        )

    def p_other(q, k, g):
        return (b_at[q] != (k + g) % 4) | (z != g)

    def gathered(q, k, group, count):
        if q == 0:
            return fwin.at[pl.ds(k * 48 + group, count)]
        return fwout.at[pl.ds(group, count), k]

    def pg_send(q, n):
        db, dz = n // 8, n % 8
        k = (b_at[q] + 8 - z) % 4
        at = gathered(q, k, core * 24 + a_at[q] * 6 + z, 1)
        return remote(
            at, at, gz_ss.at[q, db, dz], gz_rs.at[q, k, z], plane(q, (b_at[q] + db) % 4, (z + dz) % 8)
        )

    def pg_recv(q, k, g):
        at = gathered(q, k, core * 24 + a_at[q] * 6 + g, 1)
        return remote(at, at, gz_ss.at[q, 0, 0], gz_rs.at[q, k, g], partner)

    def ag_send(q, k, d):
        at = gathered(q, k, core * 24 + a_at[q] * 6, 6)
        return remote(at, at, ga_ss.at[q, d - 1, k], ga_rs.at[q, d - 1, k], a_peer[q](d))

    def cg_send(q, k):
        at = gathered(q, k, core * 24, 24)
        return remote(at, at, gc_ss.at[q, k], gc_rs.at[q, k], partner)

    def reduce_core(k):
        for q in range(2):
            core_send(q, k).wait_recv()
            def add(g, carry, q=q):
                own = bufs[q][pl.ds(k * 48 + core * 24 + g * 6, 6)].astype(F32)
                s0[q, k, pl.ds(g * 6, 6)] = (own + r0[q, k, pl.ds(g * 6, 6)].astype(F32)).astype(BF16)
                return carry
            lax.fori_loop(0, 4, add, 0)
            for d in (2, 1, 3):
                a_send(q, k, d).start()

    def reduce_a(k):
        for q in range(2):
            for d in (1, 2, 3):
                a_send(q, k, d).wait_recv()
            v = s0[q, k, pl.ds(a_at[q] * 6, 6)].astype(F32)
            for d in range(3):
                v = v + r1[q, d, k].astype(F32)
            s1[q, k] = v.astype(BF16)

            for g in range(6):
                @pl.when(p_other(q, k, g))
                def _(q=q, g=g):
                    p_send(q, k, g).start()

    def reduce_p(k):
        for q in range(2):
            @pl.when((z < 6) & ((b_at[q] + 8 - z) % 4 == k))
            def _(q=q):
                def add(n, v):
                    db, dz = n // 8, n % 8
                    remote(
                        s1.at[q, 0, 0], r3.at[q, db, dz], s3_ss.at[q, 0, 0], s3_rs.at[q, db, dz], partner
                    ).wait_recv()
                    return v + r3[q, db, dz].astype(F32)

                v = lax.fori_loop(1, 32, add, s1[q, k, z].astype(F32))
                gathered(q, k, core * 24 + a_at[q] * 6 + z, 1)[...] = v.astype(BF16)[None]

                def send(n, carry):
                    pg_send(q, n).start()
                    return carry

                lax.fori_loop(1, 32, send, 0)

    def gather_p(k):
        for q in range(2):
            for g in range(6):
                @pl.when(p_other(q, k, g))
                def _(q=q, g=g):
                    pg_recv(q, k, g).wait_recv()
            for d in (2, 1, 3):
                ag_send(q, k, d).start()

    def gather_a(k):
        for q in range(2):
            for d in (1, 2, 3):
                ag_send(q, k, d).wait_recv()
            cg_send(q, k).start()

    def out_copy(q, k):
        if q == 0:
            at = pl.ds(k * 48, 48)
            return pltpu.make_async_copy(fwin.at[at], fwin_at.at[at], wout_sems.at[q, k])
        return pltpu.make_async_copy(fwout.at[:, k], fwout_at.at[:, k], wout_sems.at[q, k])

    def gather_core(k):
        for q in range(2):
            cg_send(q, k).wait_recv()
            out_copy(q, k).start()

    def wait_early_sends():
        for q in range(2):
            for k in range(4):
                core_send(q, k).wait_send()
                for d in (1, 2, 3):
                    a_send(q, k, d).wait_send()

                for g in range(6):
                    @pl.when(p_other(q, k, g))
                    def _(q=q, k=k, g=g):
                        p_send(q, k, g).wait_send()
        for c in first + second:
            c.wait_send()

    def wait_late_sends():
        for q in range(2):
            @pl.when(z < 6)
            def _(q=q):
                def sent(n, carry):
                    pg_send(q, n).wait_send()
                    return carry

                lax.fori_loop(1, 32, sent, 0)

            for d in (1, 2, 3):
                for k in range(4):
                    ag_send(q, k, d).wait_send()

    def hidden_step(k, carry):
        cols = pl.ds(pl.multiple_of(k * C, 128), C)

        def pixel_step(b, inner):
            rows = pl.ds(pl.multiple_of(b * 128, 128), 128)
            pre = dot(ln[rows, :], w_in[cols, :], NT) + b_in[:, cols]
            d_hidden = dot(db[rows, :], w_out[:, cols], NN)
            cdf = 0.5 * (1.0 + lax.erf(pre * inv_root_two))
            pdf = jnp.exp(-0.5 * pre * pre) * inv_root_tau
            hid[rows, cols] = (pre * cdf).astype(BF16)
            d_pre = d_hidden * (cdf + pre * pdf)
            acc[4 + k] += jnp.sum(d_pre.reshape(16, 8, C), axis=0)
            dp[rows, cols] = d_pre.astype(BF16)
            return inner

        for b in range(4):
            pixel_step(b, 0)

        @pl.when(k > 0)
        def _():
            reduce_core(k - 1)

        for b in range(4, 8):
            pixel_step(b, 0)
        gw = dot(dbt[...], hid[:, cols], NN)
        bwout[pl.ds(k * 48, 48)] = (gw * factor).reshape(48, 8, C).astype(BF16)
        gi = dot(lnt[...], dp[:, cols], NN).T
        bwin[pl.ds(k * 48, 48)] = (gi * factor).reshape(48, 8, C).astype(BF16)
        for q in range(2):
            core_send(q, k).start()

        @pl.when(k > 1)
        def _():
            reduce_a(k - 2)

        return carry

    loads[2].wait()
    loads[3].wait()
    lax.fori_loop(0, 4, hidden_step, 0)

    def out_step(p, carry):
        rows = pl.ds(pl.multiple_of(p * 256, 256), 256)
        branch = dot(hid[rows, :], w_out[...], NT) + b_out[...]
        d_norm = dot(dp[rows, :], w_in[...], NN)
        acc[8] += jnp.sum((cotp[rows, :] * branch).reshape(32, 8, C), axis=0)
        for lb in range(LB):
            v = page[lb, pl.ds(p * 8 + 3, 8)].reshape(256, 128) + ls[:, lanes(lb)] * branch[:, lanes(lb)]
            for r in range(8):
                for q in range(4):
                    at = (r * 4 + q) * 8
                    outp[lb, pl.ds((p * 8 + r) * 32 + q, 8, stride=4), :] = v[at : at + 8]
        n = norm[rows, :]
        acc[1] += jnp.sum((d_norm * n).reshape(32, 8, C), axis=0)
        acc[2] += jnp.sum(d_norm.reshape(32, 8, C), axis=0)
        s = d_norm * gain[...]
        mean_s = jnp.mean(s, axis=-1, keepdims=True)
        mean_sn = jnp.mean(s * n, axis=-1, keepdims=True)
        istd = inv[rows, :]
        for lb in range(LB):
            w = lanes(lb)
            v = istd * (s[:, w] - mean_s - n[:, w] * mean_sn)
            v = v.astype(BF16).astype(F32)
            acc[0, :, w] += jnp.sum(v.reshape(32, 8, 128), axis=0)
            strips = v.reshape(8, 4, 8, 128)
            for k, u in enumerate(taps_to_points([strips[:, q] for q in range(4)])):
                dhat[lb, pl.ds(p * 8, 8), k] = u
            for r in range(8):
                for q in range(4):
                    at = (r * 4 + q) * 8
                    pf[lb, pl.ds((p * 8 + r + 8) * PW + 8 + q, 8, stride=4), :] = v[at : at + 8]
        return carry

    out_step(0, 0)
    reduce_core(3)
    out_step(1, 0)
    reduce_a(2)
    out_step(2, 0)
    reduce_p(0)
    out_step(3, 0)
    halo_pack(1)
    second = halo_copies(1)
    for c in second:
        c.start()
    reduce_a(3)

    def write_image(dst):
        def step(i, carry):
            for lb in range(LB):
                dst[i, :, lanes(lb)] = outp[lb, pl.ds(pl.multiple_of(i * 32, 8), 32), :].astype(BF16)
            return carry
        lax.fori_loop(0, 32, step, 0)

    write_image(result)
    result_copy = pltpu.make_async_copy(result, result_at, out_sems.at[0])
    result_copy.start()

    def kernel_grad(lb):
        for first_a, count in ((0, 2), (2, 2), (4, 2), (6, 1)):
            def row_step(h, sums, first_a=first_a, count=count):
                i = h * 2
                block = xu[lb, pl.ds(i + first_a, count + 1)]
                grad = dhat[lb, pl.ds(i, 2)]
                return tuple(
                    sums[n] + block[n] * grad[0] + block[n + 1] * grad[1] for n in range(count)
                )
            zero = jnp.zeros((10, 8, 128), F32)
            sums = lax.fori_loop(0, 16, row_step, (zero,) * count)
            for n in range(count):
                for k in range(10):
                    gsum[lb, (k * 8 + first_a + n) * 8 : (k * 8 + first_a + n + 1) * 8, :] = sums[n][k]

    kernel_grad(0)
    reduce_p(1)
    kernel_grad(1)
    kernel_grad(2)

    for lb in range(LB):
        gsum_rows = gsum[lb, pl.ds(0, 80, stride=8), :]
        for r in range(1, 8):
            gsum_rows = gsum_rows + gsum[lb, pl.ds(r, 80, stride=8), :]
        grads = from_points([gsum_rows[k * 8 : k * 8 + 8] for k in range(10)], 7)
        for b in range(7):
            smf[lb, pl.ds(b, 8, stride=8), :] = grads[b]
        smf[lb, pl.ds(7, 8, stride=8), :] = jnp.zeros((8, 128), F32)
        for j in range(8):
            accv[lb, j * 8 : j * 8 + 8, :] = acc[j, :, lanes(lb)]
        v = accv[lb, pl.ds(0, 8, stride=8), :]
        for r in range(1, 8):
            v = v + accv[lb, pl.ds(r, 8, stride=8), :]
        smf[lb, 56:64, :] = v
        smf[lb, 7:8, :] = jnp.sum(acc[8, :, lanes(lb)], axis=0, keepdims=True)
        sm[:, :, lanes(lb)] = (smf[lb] * factor).reshape(8, 8, 128)

    def m0():
        return remote(sm.at[pl.ds((1 - core) * 4, 4)], t0, m0_ss, m0_rs, partner)

    def m1(d):
        return remote(sa.at[(x + d) % 4], t1.at[d - 1], m1_ss.at[d - 1], m1_rs.at[d - 1], x_peer(d))

    def m2(d):
        return remote(sb, t2.at[y], m2_ss.at[d - 1], m2_rs.at[d - 1], y_peer(d))

    def m3(d):
        return remote(sc, t3.at[z], m3_ss.at[d - 1], m3_rs.at[d - 1], z_peer(d))

    def m4(d):
        at = core * 4 + x
        return remote(small.at[at], small.at[at], m4_ss.at[d - 1], m4_rs.at[d - 1], x_peer(d))

    def m5():
        at = pl.ds(core * 4, 4)
        return remote(small.at[at], small.at[at], m5_ss, m5_rs, partner)

    m0().start()

    def back_conv(lb, start, stop):
        def step(h, carry):
            i = h * 2
            outs_at = conv_rows(du, khf, lb, i)
            for q in range(4):
                for r in range(2):
                    at = pl.ds(pl.multiple_of((i + r) * 32 + q * 8, 8), 8)
                    outp[lb, pl.ds((i + r) * 32 + q, 8, stride=4), :] = outs_at[q][r] + cotp[at, lanes(lb)]
            return carry
        lax.fori_loop(start, stop, step, 0)

    gather_p(0)
    reduce_p(2)
    for c in second:
        c.wait_recv()
    halo_unpack(1)
    m0().wait_recv()
    sa[...] = sm[pl.ds(core * 4, 4)] + t0[...]
    for d in (2, 1, 3):
        m1(d).start()
    build_strips(du, None)
    reduce_p(3)
    gather_p(1)
    for d in (1, 2, 3):
        m1(d).wait_recv()
    v = sa[x] + t1[0] + t1[1] + t1[2]
    sb[...] = v
    t2[y] = v
    for d in (2, 1, 3):
        m2(d).start()
    back_conv(0, 0, 16)
    gather_a(0)
    gather_p(2)
    for d in (1, 2, 3):
        remote(sb, t2.at[(y + 4 - d) % 4], m2_ss.at[d - 1], m2_rs.at[d - 1], y_peer(d)).wait_recv()
    v = t2[0] + t2[1] + t2[2] + t2[3]
    sc[...] = v
    t3[z] = v
    for d in (4, 3, 5, 2, 6, 1, 7):
        m3(d).start()
    back_conv(1, 0, 16)
    gather_a(1)
    back_conv(2, 0, 16)
    gather_p(3)
    gather_core(0)
    gather_core(1)
    gather_a(2)
    for d in range(1, 8):
        remote(sc, t3.at[(z + 8 - d) % 8], m3_ss.at[d - 1], m3_rs.at[d - 1], z_peer(d)).wait_recv()
    v = t3[0]
    for j in range(1, 8):
        v = v + t3[j]
    small[core * 4 + x] = v
    for d in (2, 1, 3):
        m4(d).start()
    write_image(gpages)
    gpages_copy = pltpu.make_async_copy(gpages, gpages_at, out_sems.at[1])
    gpages_copy.start()
    wait_early_sends()
    gather_core(2)
    gather_a(3)
    for d in (1, 2, 3):
        at = core * 4 + (x + 4 - d) % 4
        remote(small.at[at], small.at[at], m4_ss.at[d - 1], m4_rs.at[d - 1], x_peer(d)).wait_recv()
    m5().start()
    wait_late_sends()
    at = pl.ds((1 - core) * 4, 4)
    remote(small.at[at], small.at[at], m5_ss, m5_rs, partner).wait_recv()
    small_copy = pltpu.make_async_copy(small, small_at, out_sems.at[2])
    small_copy.start()
    m0().wait_send()
    m5().wait_send()
    for d in (1, 2, 3):
        m1(d).wait_send()
        m2(d).wait_send()
        m4(d).wait_send()
    for d in range(1, 8):
        m3(d).wait_send()
    gather_core(3)
    for q in range(2):
        for k in range(4):
            cg_send(q, k).wait_send()
            out_copy(q, k).wait()
    result_copy.wait()
    gpages_copy.wait()
    small_copy.wait()


def finish(
    result_at, gpages_at, fwin_at, fwout_at, small_at,
    result_out, gpages_out, *rest_at,
):
    (
        gk_out, cb_out, gain_out, nbias_out, win_out, bin_out, wout_out, bout_out, scale_out,
        result, gpages, fwin, fwout, small, win, wout, g_kernel, g_cb, g_gain, g_nbias, g_bin, g_bout, g_scale,
        in_sems, mid_sems, out_sems, small_sems,
    ) = rest_at
    parts = 4
    win_in = [
        pltpu.make_async_copy(fwin_at.at[pl.ds(i * 48, 48)], fwin.at[pl.ds(i * 48, 48)], in_sems.at[0, i])
        for i in range(parts)
    ]
    wout_in = [
        pltpu.make_async_copy(fwout_at.at[pl.ds(i * 12, 12)], fwout.at[pl.ds(i * 12, 12)], in_sems.at[1, i])
        for i in range(parts)
    ]
    images = ((result_at, result, result_out), (gpages_at, gpages, gpages_out))
    image_in = [pltpu.make_async_copy(a, b, mid_sems.at[0, i]) for i, (a, b, _) in enumerate(images)]
    image_out = [pltpu.make_async_copy(b, c, mid_sems.at[1, i]) for i, (_, b, c) in enumerate(images)]
    win_done = [
        pltpu.make_async_copy(win.at[pl.ds(i * 384, 384)], win_out.at[pl.ds(i * 384, 384)], out_sems.at[0, i])
        for i in range(parts)
    ]
    wout_done = [
        pltpu.make_async_copy(wout.at[pl.ds(i * 96, 96)], wout_out.at[pl.ds(i * 96, 96)], out_sems.at[1, i])
        for i in range(parts)
    ]
    small_in = pltpu.make_async_copy(small_at, small, small_sems.at[7])
    small_done = [
        pltpu.make_async_copy(a, b, small_sems.at[i])
        for i, (a, b) in enumerate(
            (
                (g_kernel, gk_out), (g_cb, cb_out), (g_gain, gain_out), (g_nbias, nbias_out),
                (g_bin, bin_out), (g_bout, bout_out), (g_scale, scale_out),
            )
        )
    ]
    for c in [small_in] + win_in + wout_in + image_in:
        c.start()
    small_in.wait()
    g_kernel[...] = small[:7, :7]
    for j, ref in enumerate((g_cb, g_gain, g_nbias, g_bout)):
        ref[...] = small[7, j]
    for j in range(4):
        g_bin[j * C : j * C + C] = small[7, 4 + j]
    g_scale[...] = small[0, 7]
    for c in small_done:
        c.start()
    for i in range(parts):
        win_in[i].wait()

        def widen(g, carry):
            win[pl.ds(pl.multiple_of(g * 32, 32), 32), :] = fwin[pl.ds(g * 4, 4)].astype(F32).reshape(32, C)
            return carry

        lax.fori_loop(i * 12, i * 12 + 12, widen, 0)
        win_done[i].start()
    for i in range(parts):
        wout_in[i].wait()

        def spread(g, carry):
            for k in range(4):
                wout[pl.ds(pl.multiple_of(g * 8, 8), 8), k * C : k * C + C] = fwout[g, k].astype(F32)
            return carry

        lax.fori_loop(i * 12, i * 12 + 12, spread, 0)
        wout_done[i].start()
    for a, b in zip(image_in, image_out):
        a.wait()
        b.start()
    for c in image_out + win_done + wout_done + small_done:
        c.wait()


def shards(pages, cotangent, conv_kernel, conv_bias, norm_gain, norm_bias, w_in, b_in, w_out, b_out, layer_scale):
    vm = pl.BlockSpec(memory_space=pltpu.VMEM)
    V = pltpu.VMEM
    D = pltpu.SemaphoreType.DMA
    scratch = [
        V((LB, 48 * PW, 128), F32),
        V((LB, 38, 10, 8, 128), F32),
        V((LB, 38, 4, 8, 128), F32),
        V((LB, 38, 10, 8, 128), F32),
        V((PIX, C), F32),
        V((PIX, C), F32),
        V((PIX, 128), F32),
        V((PIX, C), F32),
        V((PIX, C), BF16),
        V((C, PIX), BF16),
        V((PIX, C), BF16),
        V((C, PIX), BF16),
        V((PIX, HID), BF16),
        V((PIX, HID), BF16),
        V((LB, ROWS, 10, 8, 128), F32),
        V((LB, PIX, 128), F32),
        V((49, 8, C), F32),
        V((70, 8, C), F32), V((70, 8, C), F32),
        V((9, 8, C), F32), V((LB, 64, 128), F32),
        V((LB, 640, 128), F32), V((LB, 64, 128), F32),
        V((2, 2, 3, 32, C), BF16), V((2, 2, 3, 32, C), BF16),
        V((2, 2, 3, 32, C), BF16), V((2, 2, 3, 32, C), BF16),
        V((2, 2, 2, 3, 8, C), BF16), V((2, 2, 2, 3, 8, C), BF16),
        V((192, 8, C), BF16), V((192, 8, C), BF16),
        V((2, 4, 24, 8, C), BF16), V((2, 4, 24, 8, C), BF16),
        V((2, 3, 4, 6, 8, C), BF16), V((2, 4, 6, 8, C), BF16),
        V((2, 4, 8, 8, C), BF16),
        V((8, 8, C), F32), V((4, 8, C), F32), V((4, 8, C), F32), V((3, 8, C), F32),
        V((8, C), F32), V((4, 8, C), F32), V((8, C), F32), V((8, 8, C), F32),
        V((1, C), F32), V((1, C), F32), V((1, C), F32), V((1, HID), F32), V((1, C), F32), V((1, C), F32),
        D((2, 8)), D((2, 8)),
        D((2, 4)), D((2, 4)), D((2, 3, 4)), D((2, 3, 4)), D((2, 4, 6)), D((2, 4, 8)),
        D((2, 4, 8)), D((2, 4, 8)), D((2, 3, 4)), D((2, 3, 4)), D((2, 4)), D((2, 4)),
        D, D, D((3,)), D((3,)), D((3,)), D((3,)), D((7,)), D((7,)), D((3,)), D((3,)), D, D,
    ]
    image = jax.ShapeDtypeStruct((ROWS, COLS, C), BF16)
    pixels = PIX * lax.axis_size("gy") * lax.axis_size("gx") * lax.axis_size("rep")
    factor = float(pixels) ** (-0.5)
    hbm = pl.BlockSpec(memory_space=pl.ANY)
    mid = (
        image, image, jax.ShapeDtypeStruct((192, 8, C), BF16), jax.ShapeDtypeStruct((48, 4, 8, C), BF16),
        jax.ShapeDtypeStruct((8, 8, C), F32),
    )
    own = [V(v.shape, v.dtype) for v in mid]
    weights = [V((HID, C), BF16), V((C, HID), BF16)]
    mid = pl.pallas_call(
        functools.partial(body, factor),
        out_shape=mid,
        in_specs=[hbm, hbm, vm, vm, vm, vm, hbm, vm, hbm, vm, vm],
        out_specs=(hbm,) * 5,
        scratch_shapes=own[:2] + weights + own + [D((4,)), D((3,)), D((2, 4))] + scratch,
        compiler_params=pltpu.CompilerParams(
            collective_id=0, has_side_effects=True, vmem_limit_bytes=63 * 1024 * 1024
        ),
        name="block",
    )(
        pages[0], cotangent[0], conv_kernel, conv_bias, norm_gain, norm_bias,
        w_in, b_in, w_out, b_out, layer_scale,
    )
    row = jax.ShapeDtypeStruct((C,), F32)
    outs = pl.pallas_call(
        finish,
        out_shape=(
            image, image, jax.ShapeDtypeStruct((7, 7, C), F32), row, row, row,
            jax.ShapeDtypeStruct((HID, C), F32), jax.ShapeDtypeStruct((HID,), F32),
            jax.ShapeDtypeStruct((C, HID), F32), row, row,
        ),
        in_specs=[hbm] * 5,
        out_specs=(hbm,) * 11,
        scratch_shapes=own + [V((HID, C), F32), V((C, HID), F32), V((7, 7, C), F32)]
        + [V((C,), F32)] * 3 + [V((HID,), F32), V((C,), F32), V((C,), F32)]
        + [D((2, 4)), D((2, 2)), D((2, 4)), D((8,))],
        compiler_params=pltpu.CompilerParams(vmem_limit_bytes=63 * 1024 * 1024),
        name="finish",
    )(*mid)
    return (outs[0][None], outs[1][None]) + tuple(outs[2:])


def solution(mesh):
    tile = P("rep", "gy", "gx", None)
    return jax.shard_map(
        shards,
        mesh=mesh,
        in_specs=(tile, tile) + (P(),) * 9,
        out_specs=(tile, tile) + (P(),) * 9,
        check_vma=False,
    )
```
